512 devices in a mesh: uly: 32 (over y, z_hi, core), blk: 16 (over z_lo, x).
Axes of the slice: x: 4, y: 8, z: 8 (z_hi: 2, z_lo: 4; z = z_hi * 4 + z_lo), core: 2. Of those that a mesh axis runs over, the one named last changes fastest.
Arguments:
- queries: bfloat16 [65536, 32, 128], P(('blk', 'uly')), may hold values from -6 to 6
- keys: bfloat16 [65536, 8, 128], P(('blk', 'uly')), may hold values from -6 to 6
- values: bfloat16 [65536, 8, 128], P(('blk', 'uly')), may hold values from -6 to 6
- grad_out: bfloat16 [65536, 32, 128], P(('blk', 'uly')), may hold values from -6 to 6
- lse: float32 [32, 65536], P('uly'), may hold values from 4 to 6
- delta: float32 [32, 65536], P('uly'), may hold values from -18 to 18
- block_keys: int32 [512, 5], replicated, may hold values from -1 to 511, as said below
Outputs:
- grad_queries: bfloat16 [65536, 32, 128], P(('blk', 'uly'))
- grad_keys: bfloat16 [65536, 8, 128], P(('blk', 'uly'))
- grad_values: bfloat16 [65536, 8, 128], P(('blk', 'uly'))
The draws below stay inside these ranges and needn't reach their ends.
Inputs may be any that keep to these rules, and one draw needn't show every extreme that they name: `block_keys`: query block b lists itself first, then 5 - 1 distinct earlier blocks c with c >= 32 * (b // 32 - 1); entries are -1 only where fewer earlier blocks exist, after the listed ones.
All inputs are finite; a program needn't handle non-finite values.
Results may differ from the reference program's by a relative error of at most 0.0053.
Values may be sent and summed in bfloat16 or wider, within the bound.
A program may use at most 128 MiB of HBM per device.

```python
import math
import jax
import jax.numpy as jnp
from jax import lax

HEADS = 32
KVH = 8
HD = 128
BLOCK = 128
KSEL = 5
SLAB_BLOCKS = 32
SEQ = 65536
NBLOCKS = 512


def draw_block_keys(key, part):
    block_ids = jnp.arange(NBLOCKS, dtype=jnp.int32)
    span = 2 * SLAB_BLOCKS - 1
    offsets = jnp.arange(span, dtype=jnp.int32)
    lowest = jnp.maximum(0, (block_ids // SLAB_BLOCKS - 1) * SLAB_BLOCKS)
    candidate = block_ids[:, None] - 1 - offsets[None, :]
    usable = candidate >= lowest[:, None]
    raw_scores = jax.random.randint(key, (NBLOCKS, span), 0, 1 << 20, dtype=jnp.int32)
    ranked = jnp.where(usable, raw_scores * (2 * SLAB_BLOCKS) + offsets[None, :], -1)
    best, where_best = lax.top_k(ranked, KSEL - 1)
    picked = jnp.where(best >= 0, block_ids[:, None] - 1 - where_best.astype(jnp.int32), -1)
    return jnp.concatenate([block_ids[:, None], picked], axis=1).astype(jnp.int32)


def block_levels(rng, dims, shards, least, high):
    loudness = 1.0
    for dim, shards_of in shards:
        heights = jax.random.uniform(jax.random.fold_in(jax.random.fold_in(rng, 6), dim), (shards_of,), jnp.float32, least / len(shards), high / len(shards))
        loudness = loudness * jnp.repeat(jnp.exp(heights), dims[dim] // shards_of).reshape((-1,) + (1,) * (len(dims) - 1 - dim))
    return loudness


def scatter_about(stream_key, dims, scale, reach, cuts=(), held_as=jnp.bfloat16):
    drawn = scale * jax.random.normal(stream_key, dims, jnp.float32)
    if cuts:
        drawn = drawn * block_levels(stream_key, dims, cuts, -0.22, 0.18)
    return jnp.clip(drawn, -reach, reach).astype(held_as)


def setup_inputs(seed: int = 0) -> dict:
    splits = jax.random.split(jax.random.key(seed), 8)
    return {
        "queries": scatter_about(splits[0], (SEQ, HEADS, HD), 1.0, 6.0, ((0, 512),)),
        "keys": scatter_about(splits[1], (SEQ, KVH, HD), 1.0, 6.0, ((0, 512),)),
        "values": scatter_about(splits[2], (SEQ, KVH, HD), 1.0, 6.0, ((0, 512),)),
        "grad_out": scatter_about(splits[3], (SEQ, HEADS, HD), 1.0, 6.0, ((0, 512),)),
        "lse": jnp.clip(4.0 + 2.0 * jax.random.uniform(splits[4], (HEADS, SEQ), jnp.float32) ** block_levels(splits[4], (HEADS, SEQ), ((0, 32),), -0.2, 0.2), 4.0, 6.0),
        "delta": scatter_about(splits[5], (HEADS, SEQ), 3.0, 18.0, ((0, 32),), jnp.float32),
        "block_keys": draw_block_keys(jax.random.fold_in(splits[7], 71), 0),
    }


def block_grads(query_rows, dout_rows, lse_rows, delta_rows, key_blocks, value_blocks, block_index, block_valid, block_diag, per_step):
    query_blocks = block_index.shape[0]
    width = key_blocks.shape[1]
    head_dim = key_blocks.shape[2]
    head_count = query_rows.shape[1]
    select = block_index.shape[1]
    step_count = query_blocks // per_step
    score_scale = 1.0 / math.sqrt(head_dim)
    query_steps = query_rows.reshape(step_count, per_step, width, head_count, head_dim)
    dout_steps = dout_rows.reshape(step_count, per_step, width, head_count, head_dim)
    lse_steps = lse_rows.reshape(head_count, step_count, per_step, width).transpose(1, 2, 0, 3)
    delta_steps = delta_rows.reshape(head_count, step_count, per_step, width).transpose(1, 2, 0, 3)
    safe_index = jnp.where(block_valid, block_index, 0).astype(jnp.int32).reshape(step_count, per_step, select)
    valid_steps = block_valid.reshape(step_count, per_step, select)
    diag_steps = block_diag.reshape(step_count, per_step, select)
    positions = jnp.arange(width, dtype=jnp.int32)
    causal = positions[None, :] <= positions[:, None]

    def advance(carry, inputs):
        key_acc, value_acc = carry
        query_part, dout_part, lse_part, delta_part, index_part, valid_part, diag_part = inputs
        key_part = key_blocks[index_part].astype(jnp.float32)
        value_part = value_blocks[index_part].astype(jnp.float32)
        query_wide = query_part.astype(jnp.float32)
        dout_wide = dout_part.astype(jnp.float32)
        scores = jnp.einsum('pthd,pjsd->phtjs', query_wide, key_part) * score_scale
        allowed = valid_part[:, None, None, :, None] & (jnp.logical_not(diag_part)[:, None, None, :, None] | causal[None, None, :, None, :])
        probs = jnp.where(allowed, jnp.exp(scores - lse_part[:, :, :, None, None]), 0.0)
        dprobs = jnp.einsum('pthd,pjsd->phtjs', dout_wide, value_part)
        dscores = probs * (dprobs - delta_part[:, :, :, None, None])
        probs_low = probs.astype(jnp.bfloat16).astype(jnp.float32)
        dscores_low = dscores.astype(jnp.bfloat16).astype(jnp.float32)
        grad_query = jnp.einsum('phtjs,pjsd->pthd', dscores_low, key_part) * score_scale
        grad_value = jnp.einsum('phtjs,pthd->pjsd', probs_low, dout_wide)
        grad_key = jnp.einsum('phtjs,pthd->pjsd', dscores_low, query_wide) * score_scale
        flat_index = index_part.reshape(-1)
        key_acc = key_acc.at[flat_index].add(grad_key.reshape(-1, width, head_dim))
        value_acc = value_acc.at[flat_index].add(grad_value.reshape(-1, width, head_dim))
        return ((key_acc, value_acc), grad_query)
    start = jnp.zeros((key_blocks.shape[0], width, head_dim), jnp.float32)
    (key_acc, value_acc), grad_query = lax.scan(advance, (start, start), (query_steps, dout_steps, lse_steps, delta_steps, safe_index, valid_steps, diag_steps))
    return (grad_query.reshape(query_blocks * width, head_count, head_dim), key_acc, value_acc)

def reference(queries, keys, values, grad_out, lse, delta, block_keys):
    seq_len = queries.shape[0]
    block_total = seq_len // BLOCK
    group = HEADS // KVH
    per_step = math.gcd(block_total, max(1, 512 // BLOCK))
    block_ids = jnp.arange(block_total, dtype=jnp.int32)
    block_valid = block_keys >= 0
    block_diag = block_keys == block_ids[:, None]

    def one_group(kv_index):
        query_rows = lax.dynamic_slice_in_dim(queries, kv_index * group, group, 1)
        dout_rows = lax.dynamic_slice_in_dim(grad_out, kv_index * group, group, 1)
        lse_rows = lax.dynamic_slice_in_dim(lse, kv_index * group, group, 0)
        delta_rows = lax.dynamic_slice_in_dim(delta, kv_index * group, group, 0)
        key_blocks = lax.dynamic_slice_in_dim(keys, kv_index, 1, 1).reshape(block_total, BLOCK, HD)
        value_blocks = lax.dynamic_slice_in_dim(values, kv_index, 1, 1).reshape(block_total, BLOCK, HD)
        return block_grads(query_rows, dout_rows, lse_rows, delta_rows, key_blocks, value_blocks, block_keys, block_valid, block_diag, per_step)
    grad_query, grad_key, grad_value = lax.map(one_group, jnp.arange(KVH, dtype=jnp.int32))
    grad_queries = grad_query.transpose(1, 0, 2, 3).reshape(seq_len, HEADS, HD).astype(jnp.bfloat16)
    grad_keys = grad_key.reshape(KVH, seq_len, HD).transpose(1, 0, 2).astype(jnp.bfloat16)
    grad_values = grad_value.reshape(KVH, seq_len, HD).transpose(1, 0, 2).astype(jnp.bfloat16)
    return (grad_queries, grad_keys, grad_values)
```

```python
import functools
import math

import jax
import jax.numpy as jnp
from jax import lax
from jax.experimental import pallas as pl
from jax.experimental.pallas import tpu as pltpu
from jax.sharding import PartitionSpec as P

BLOCK = 128
OFF = -1e30


def grads_kernel(scale, idx, bias, lse, delta, q, do, keys, vals, dq, dk, dv):
    step = pl.program_id(0)
    select = idx.shape[1]
    rows = q.shape[1]
    heads = rows // BLOCK

    @pl.when(step == 0)
    def _():
        dk[...] = jnp.zeros_like(dk)
        dv[...] = jnp.zeros_like(dv)

    places = [idx[step, j] for j in range(select)]
    kcat = jnp.concatenate([keys[c] for c in places], 0)
    vcat = jnp.concatenate([vals[c] for c in places], 0)
    qb, dob = q[0], do[0]
    nt = (((1,), (1,)), ((), ()))
    nn = (((1,), (0,)), ((), ()))
    s = lax.dot_general(kcat, qb, nt, preferred_element_type=jnp.float32)
    dp = lax.dot_general(vcat, dob, nt, preferred_element_type=jnp.float32)
    lse_row, delta_row = lse[0], delta[0]
    probs, dscores = [], []
    for j in range(select):
        part = slice(j * BLOCK, (j + 1) * BLOCK)
        p = jnp.exp(s[part] * scale - (lse_row - bias[step, j]))
        if j == 0:
            key_at = lax.broadcasted_iota(jnp.int32, (BLOCK, rows), 0)
            query_at = lax.broadcasted_iota(jnp.int32, (BLOCK, rows), 1) // heads
            p = jnp.where(key_at <= query_at, p, 0.0)
        ds = p * (dp[part] - delta_row)
        probs.append(p.astype(jnp.bfloat16))
        dscores.append(ds.astype(jnp.bfloat16))
    pcat = jnp.concatenate(probs, 0)
    dscat = jnp.concatenate(dscores, 0)
    dv_part = lax.dot_general(pcat, dob, nn, preferred_element_type=jnp.float32)
    dk_part = lax.dot_general(dscat, qb, nn, preferred_element_type=jnp.float32)
    dqt = lax.dot_general(kcat.T, dscat, nn, preferred_element_type=jnp.float32)
    dq[0] = (dqt * scale).T.astype(jnp.bfloat16)
    for j, c in enumerate(places):
        part = slice(j * BLOCK, (j + 1) * BLOCK)
        dk[c] += dk_part[part] * scale
        dv[c] += dv_part[part]


def local_grads(idx, bias, lse, delta, q, do, keys, vals):
    steps, rows, hd = q.shape
    places = keys.shape[0]
    select = idx.shape[1]
    row = pl.BlockSpec((1, 1, rows), lambda i, *_: (i, 0, 0))
    tile = pl.BlockSpec((1, rows, hd), lambda i, *_: (i, 0, 0))
    whole = pl.BlockSpec(
        (places, BLOCK, hd), lambda i, *_: (0, 0, 0), pipeline_mode=pl.Buffered(1)
    )
    acc = jax.ShapeDtypeStruct((places, BLOCK, hd), jnp.float32)
    return pl.pallas_call(
        functools.partial(grads_kernel, 1.0 / math.sqrt(hd)),
        out_shape=(jax.ShapeDtypeStruct(q.shape, jnp.bfloat16), acc, acc),
        grid_spec=pltpu.PrefetchScalarGridSpec(
            num_scalar_prefetch=2,
            grid=(steps,),
            in_specs=[row, row, tile, tile, whole, whole],
            out_specs=(tile, whole, whole),
        ),
        compiler_params=pltpu.CompilerParams(vmem_limit_bytes=48 << 20),
        cost_estimate=pl.CostEstimate(
            flops=steps * 10 * rows * select * BLOCK * hd,
            bytes_accessed=4 * places * BLOCK * hd * 3,
            transcendentals=steps * rows * select * BLOCK,
        ),
        name="grads",
    )(idx, bias, lse, delta, q, do, keys, vals)


def shards(queries, keys, values, grad_out, lse, delta, block_keys):
    uly = lax.axis_size("uly")
    tokens, heads, hd = queries.shape
    kvh = keys.shape[1]
    group = heads // kvh
    fold = uly // kvh
    u, slab = lax.axis_index("uly"), lax.axis_index("blk")
    blks = lax.axis_size("blk")
    ys = [[y * fold + r for y in range(kvh)] for r in range(fold)]
    rs = [[y * fold + r for r in range(fold)] for y in range(kvh)]

    def over(x, groups):
        return lax.all_to_all(
            x, "uly", split_axis=0, concat_axis=0, axis_index_groups=groups, tiled=True
        )

    def by_group(x):
        return x.reshape(tokens, kvh, group, hd).transpose(1, 0, 2, 3)

    q = over(by_group(queries), ys).reshape(kvh, tokens * group, hd)
    do = over(by_group(grad_out), ys).reshape(kvh, tokens * group, hd)

    def gathered(x):
        quarter = over(x.transpose(1, 0, 2), ys)
        own = lax.all_gather(
            quarter, "uly", axis=0, axis_index_groups=rs, tiled=True
        )
        prev = lax.ppermute(own, "blk", [(i, i + 1) for i in range(blks - 1)])
        return jnp.concatenate([prev, own], 0)

    k_all, v_all = gathered(keys), gathered(values)

    slab_len = uly * tokens

    def rows_of(x):
        mine = lax.dynamic_slice_in_dim(x, slab * slab_len, slab_len, 1)
        mine = mine.reshape(kvh, fold, tokens).transpose(1, 0, 2)
        mine = over(mine, rs).reshape(group, kvh, tokens)
        return mine.transpose(1, 2, 0).reshape(kvh, 1, tokens * group)

    lse_rows, delta_rows = rows_of(lse), rows_of(delta)

    own_blocks = lax.dynamic_slice_in_dim(block_keys, slab * uly, uly, 0)
    own_blocks = lax.dynamic_index_in_dim(
        own_blocks.reshape(kvh, fold, -1), u % fold, 1, keepdims=False
    )
    own_at = jnp.where(own_blocks >= 0, own_blocks, own_blocks[:, :1])
    rel = own_at - (slab - 1) * uly
    part, home = rel // uly, rel % uly
    idx = part * uly + (home % fold) * kvh + home // fold
    bias = jnp.where(own_blocks >= 0, 0.0, OFF).astype(jnp.float32)

    dq, dk, dv = local_grads(idx, bias, lse_rows, delta_rows, q, do, k_all, v_all)

    grad_q = over(dq.reshape(kvh, tokens, group, hd), ys)
    grad_q = grad_q.transpose(1, 0, 2, 3).reshape(tokens, heads, hd)

    def sent_home(acc):
        back = lax.ppermute(
            acc[:uly].astype(jnp.bfloat16), "blk", [(i + 1, i) for i in range(blks - 1)]
        )
        total = (acc[uly:] + back).astype(jnp.bfloat16)
        parts = over(total, rs).reshape(fold, kvh, tokens, hd)
        summed = parts.astype(jnp.float32).sum(0).astype(jnp.bfloat16)
        return over(summed, ys).transpose(1, 0, 2)

    return grad_q, sent_home(dk), sent_home(dv)


def solution(mesh):
    data = P(("blk", "uly"), None, None)
    return jax.shard_map(
        shards,
        mesh=mesh,
        in_specs=(data, data, data, data, P("uly", None), P("uly", None), P()),
        out_specs=(data, data, data),
        check_vma=False,
    )
```

```python
import functools
import math

import jax
import jax.numpy as jnp
from jax import lax
from jax.experimental import pallas as pl
from jax.experimental.pallas import tpu as pltpu
from jax.sharding import PartitionSpec as P

BLOCK = 128
OFF = -1e30
MESH = pl.DeviceIdType.MESH
NEAR_FIRST = (0, 1, 7, 2, 6, 3, 5, 4)


class Place:
    def __init__(self, uly, blks, rows):
        self.fold = uly // rows
        self.rows = rows
        self.u, self.slab = lax.axis_index("uly"), lax.axis_index("blk")
        self.y, self.r = self.u // self.fold, self.u % self.fold
        self.z, self.c = self.r // 2, self.r % 2
        self.first, self.last = self.slab == 0, self.slab == blks - 1
        self.core = self.at(self.z * 2 + 1 - self.c)
        self.other = self.at((1 - self.z) * 2 + self.c)
        self.cross = self.at((1 - self.z) * 2 + 1 - self.c)
        self.after, self.before = {"blk": self.slab + 1}, {"blk": self.slab - 1}

    def at(self, r):
        return {"uly": self.y * self.fold + r}

    def row(self, y):
        return {"uly": y * self.fold + self.r}

    def y_at(self, distance):
        return (self.y + distance) % self.rows

    def meet(self):
        barrier = pltpu.get_barrier_semaphore()

        def greet(device):
            pl.semaphore_signal(barrier, inc=1, device_id=device, device_id_type=MESH)

        for d in range(1, self.rows):
            greet(self.row(self.y_at(d)))
        for device in (self.core, self.other, self.cross):
            greet(device)
        pl.when(jnp.logical_not(self.last))(lambda: greet(self.after))
        pl.when(jnp.logical_not(self.first))(lambda: greet(self.before))
        ends = self.first.astype(jnp.int32) + self.last.astype(jnp.int32)
        pl.semaphore_wait(barrier, self.rows + 4 - ends)


def remote(src, dst, sems, i, device):
    return pltpu.make_async_remote_copy(
        src_ref=src,
        dst_ref=dst,
        send_sem=sems[0].at[i],
        recv_sem=sems[1].at[i],
        device_id=device,
        device_id_type=MESH,
    )


def pair(n):
    return [pltpu.SemaphoreType.DMA((n,)), pltpu.SemaphoreType.DMA((n,))]


def inbound_kernel(uly, blks, q, do, kv, lse, delta, q_all, do_all, kv_all, lse_all, delta_all, *sems):
    rows = kv.shape[0]
    q_s, do_s, kv_s, z_s, x_s, c_s, l_s, e_s = [sems[2 * i : 2 * i + 2] for i in range(8)]
    own = sems[16]
    me = Place(uly, blks, rows)
    y, r, z, c = me.y, me.r, me.z, me.c
    has_after, has_before = jnp.logical_not(me.last), jnp.logical_not(me.first)
    me.meet()

    locals_ = [
        pltpu.make_async_copy(kv.at[y], kv_all.at[c, 1, z, y], own.at[0]),
        pltpu.make_async_copy(q.at[:, y], q_all.at[y], own.at[1]),
        pltpu.make_async_copy(do.at[:, y], do_all.at[y], own.at[2]),
        pltpu.make_async_copy(lse.at[r], lse_all.at[r], own.at[3]),
        pltpu.make_async_copy(delta.at[r], delta_all.at[r], own.at[4]),
    ]
    sends = []
    for d in range(1, rows):
        t = me.y_at(d)
        sends.append(remote(kv.at[t], kv_all.at[c, 1, z, y], kv_s, d, me.row(t)))
    for d in range(1, rows):
        t = me.y_at(d)
        sends.append(remote(q.at[:, t], q_all.at[y], q_s, d, me.row(t)))
        sends.append(remote(do.at[:, t], do_all.at[y], do_s, d, me.row(t)))
    for i in range(1, me.fold):
        t = (r + i) % me.fold
        sends.append(remote(lse.at[t], lse_all.at[r], l_s, i, me.at(t)))
        sends.append(remote(delta.at[t], delta_all.at[r], e_s, i, me.at(t)))
    for copy in locals_ + sends:
        copy.start()

    def from_row(d):
        place = kv_all.at[c, 1, z, me.y_at(rows - d)]
        return remote(place, place, kv_s, d, me.core)

    def to_other(d):
        place = kv_all.at[c, 1, z, me.y_at(rows - d)]
        return remote(place, place, z_s, d, me.other)

    def from_other(d):
        place = kv_all.at[c, 1, 1 - z, me.y_at(rows - d)]
        return remote(place, place, z_s, d, me.other)

    def to_after(d, zz, i):
        t = me.y_at(rows - d)
        return remote(kv_all.at[c, 1, zz, t], kv_all.at[c, 0, zz, t], x_s, i, me.after)

    def from_before(d, zz, i):
        place = kv_all.at[c, 0, zz, me.y_at(rows - d)]
        return remote(place, place, x_s, i, me.before)

    def to_core(d, part, zz, i):
        place = kv_all.at[c, part, zz, me.y_at(rows - d)]
        return remote(place, place, c_s, i, me.core)

    def from_core(d, part, zz, i):
        place = kv_all.at[1 - c, part, zz, me.y_at(rows - d)]
        return remote(place, place, c_s, i, me.core)

    for d in NEAR_FIRST:
        if d == 0:
            locals_[0].wait()
        else:
            from_row(d).wait_recv()
        to_other(d).start()
        pl.when(has_after)(lambda: to_after(d, z, d).start())
        to_core(d, 1, z, d).start()
    for d in NEAR_FIRST:
        from_other(d).wait_recv()
        pl.when(has_after)(lambda: to_after(d, 1 - z, rows + d).start())
        to_core(d, 1, 1 - z, rows + d).start()

        @pl.when(has_before)
        def _():
            from_before(d, z, d).wait_recv()
            to_core(d, 0, z, 2 * rows + d).start()

    @pl.when(has_before)
    def _():
        for d in NEAR_FIRST:
            from_before(d, 1 - z, rows + d).wait_recv()
            to_core(d, 0, 1 - z, 3 * rows + d).start()

    for copy in sends:
        copy.wait_send()
    for d in range(1, rows):
        q_piece, do_piece = q_all.at[me.y_at(rows - d)], do_all.at[me.y_at(rows - d)]
        remote(q_piece, q_piece, q_s, d, me.core).wait_recv()
        remote(do_piece, do_piece, do_s, d, me.core).wait_recv()
    for i in range(1, me.fold):
        t = (r + me.fold - i) % me.fold
        remote(lse_all.at[t], lse_all.at[t], l_s, i, me.core).wait_recv()
        remote(delta_all.at[t], delta_all.at[t], e_s, i, me.core).wait_recv()
    for copy in locals_[1:]:
        copy.wait()
    for d in range(rows):
        to_other(d).wait_send()
        for zz, base in ((z, 0), (1 - z, rows)):
            pl.when(has_after)(lambda: to_after(d, zz, base + d).wait_send())
            to_core(d, 1, zz, base + d).wait_send()
            from_core(d, 1, zz, base + d).wait_recv()

            @pl.when(has_before)
            def _():
                to_core(d, 0, zz, 2 * rows + base + d).wait_send()
                from_core(d, 0, zz, 2 * rows + base + d).wait_recv()


def inbound(uly, blks, q, do, kv, lse, delta):
    tokens, rows, group, hd = q.shape
    any_ = pl.BlockSpec(memory_space=pltpu.HBM)
    parts = jax.ShapeDtypeStruct((rows, tokens, group, hd), q.dtype)
    every = jax.ShapeDtypeStruct((2, 2, 2) + kv.shape, kv.dtype)
    scalars = jax.ShapeDtypeStruct(lse.shape, lse.dtype)
    return pl.pallas_call(
        functools.partial(inbound_kernel, uly, blks),
        out_shape=(parts, parts, every, scalars, scalars),
        in_specs=[any_] * 5,
        out_specs=(any_,) * 5,
        scratch_shapes=pair(rows) * 4
        + pair(2 * rows)
        + pair(4 * rows)
        + pair(4) * 2
        + [pltpu.SemaphoreType.DMA((5,))],
        compiler_params=pltpu.CompilerParams(collective_id=0, has_side_effects=True),
        name="inbound",
    )(q, do, kv, lse, delta)


def outbound_kernel(uly, blks, dq, mine, theirs, grad_q, home, from_c, to_x, from_x, to_z, from_z, total, to_y, *sems):
    rows = dq.shape[0]
    q_s, c_s, x_s, z_s, y_s = [sems[2 * i : 2 * i + 2] for i in range(5)]
    own = sems[10]
    me = Place(uly, blks, rows)
    y, z = me.y, me.z
    has_after, has_before = jnp.logical_not(me.last), jnp.logical_not(me.first)
    me.meet()

    def core(part, zz, order, d):
        t = me.y_at(d)
        i = (part * 2 + order) * rows + d
        return remote(theirs.at[part, zz, t], from_c.at[part, zz, t], c_s, i, me.core)

    def before(zz, order, d):
        t = me.y_at(d)
        return remote(to_x.at[zz, t], from_x.at[zz, t], x_s, order * rows + d, me.before)

    def other(d):
        t = me.y_at(d)
        return remote(to_z.at[t], from_z.at[t], z_s, d, me.other)

    ways = ((1 - z, 0), (z, 1))
    for part in (0, 1):
        for zz, order in ways:
            for d in range(rows):
                core(part, zz, order, d).start()
    keep = pltpu.make_async_copy(dq.at[y], grad_q.at[:, y], own.at[0])
    keep.start()
    sends = []
    for d in range(1, rows):
        t = me.y_at(d)
        sends.append(remote(dq.at[t], grad_q.at[:, y], q_s, d, me.row(t)))
        sends[-1].start()

    for zz, order in ways:

        @pl.loop(0, rows)
        def _(d):
            t = me.y_at(d)
            core(0, zz, order, d).wait_recv()

            @pl.when(has_before)
            def _():
                to_x[zz, t] = (mine[0, zz, t] + from_c[0, zz, t]).astype(jnp.bfloat16)
                before(zz, order, d).start()

    def summed(zz, order, d, store):
        t = me.y_at(d)
        core(1, zz, order, d).wait_recv()

        @pl.when(has_after)
        def _():
            before(zz, order, d).wait_recv()
            store(t, mine[1, zz, t] + from_c[1, zz, t] + from_x[zz, t])

        @pl.when(me.last)
        def _():
            store(t, mine[1, zz, t] + from_c[1, zz, t])

    @pl.loop(0, rows)
    def _(d):
        def store(t, x):
            to_z[t] = x.astype(jnp.bfloat16)

        summed(1 - z, 0, d, store)
        other(d).start()

    def back(d):
        t = me.y_at(d)
        return remote(to_y.at[t], home.at[y], y_s, d, me.row(t))

    @pl.loop(0, rows)
    def _(d):
        def store(t, x):
            total[...] = x

        summed(z, 1, d, store)
        other(d).wait_recv()
        t = me.y_at(d)
        to_y[t] = (total[...] + from_z[t]).astype(jnp.bfloat16)
        pl.when(d > 0)(lambda: back(d).start())

    last = pltpu.make_async_copy(to_y.at[y], home.at[y], own.at[1])
    last.start()
    for d in range(rows):
        for part in (0, 1):
            for zz, order in ways:
                core(part, zz, order, d).wait_send()
        for zz, order in ways:
            pl.when(has_before)(lambda: before(zz, order, d).wait_send())
        other(d).wait_send()
    for d in range(1, rows):
        t = me.y_at(rows - d)
        sends[d - 1].wait_send()
        remote(dq.at[t], grad_q.at[:, t], q_s, d, me.core).wait_recv()
        back(d).wait_send()
        remote(to_y.at[t], home.at[t], y_s, d, me.core).wait_recv()
    keep.wait()
    last.wait()


def outbound(uly, blks, dq, mine, theirs):
    rows, tokens, group, hd = dq.shape
    hbm, vmem = pl.BlockSpec(memory_space=pltpu.HBM), pl.BlockSpec(memory_space=pltpu.VMEM)
    piece = mine.shape[3:]
    low = jnp.bfloat16
    return pl.pallas_call(
        functools.partial(outbound_kernel, uly, blks),
        out_shape=(
            jax.ShapeDtypeStruct((tokens, rows, group, hd), low),
            jax.ShapeDtypeStruct((rows,) + piece, low),
        ),
        in_specs=[hbm, vmem, hbm],
        out_specs=(hbm, hbm),
        scratch_shapes=[
            pltpu.VMEM(mine.shape, low),
            pltpu.VMEM(mine.shape[1:], low),
            pltpu.VMEM(mine.shape[1:], low),
            pltpu.VMEM((rows,) + piece, low),
            pltpu.VMEM((rows,) + piece, low),
            pltpu.VMEM(piece, jnp.float32),
            pltpu.VMEM((rows,) + piece, low),
        ]
        + pair(rows)
        + pair(4 * rows)
        + pair(2 * rows)
        + pair(rows) * 2
        + [pltpu.SemaphoreType.DMA((2,))],
        compiler_params=pltpu.CompilerParams(
            collective_id=1, has_side_effects=True, vmem_limit_bytes=32 << 20
        ),
        name="outbound",
    )(dq, mine, theirs)


def grads_kernel(scale, idx, bias, half, lse, delta, q, do, kv, dq, mine, theirs, acc):
    step = pl.program_id(0)
    select = idx.shape[1]
    rows = q.shape[1]
    heads = rows // BLOCK

    @pl.when(step == 0)
    def _():
        acc[...] = jnp.zeros_like(acc)

    places = [idx[step, j] for j in range(select)]
    kcat = jnp.concatenate([kv[c, 0] for c in places], 0)
    vcat = jnp.concatenate([kv[c, 1] for c in places], 0)
    qb, dob = q[0], do[0]
    nt = (((1,), (1,)), ((), ()))
    nn = (((1,), (0,)), ((), ()))
    s = lax.dot_general(kcat, qb, nt, preferred_element_type=jnp.float32)
    dp = lax.dot_general(vcat, dob, nt, preferred_element_type=jnp.float32)
    lse_row, delta_row = lse[0], delta[0]
    probs, dscores = [], []
    for j in range(select):
        part = slice(j * BLOCK, (j + 1) * BLOCK)
        p = jnp.exp(s[part] * scale - (lse_row - bias[step, j]))
        if j == 0:
            key_at = lax.broadcasted_iota(jnp.int32, (BLOCK, rows), 0)
            query_at = lax.broadcasted_iota(jnp.int32, (BLOCK, rows), 1) // heads
            p = jnp.where(key_at <= query_at, p, 0.0)
        ds = p * (dp[part] - delta_row)
        probs.append(p.astype(jnp.bfloat16))
        dscores.append(ds.astype(jnp.bfloat16))
    pcat = jnp.concatenate(probs, 0)
    dscat = jnp.concatenate(dscores, 0)
    dv_part = lax.dot_general(pcat, dob, nn, preferred_element_type=jnp.float32)
    dk_part = lax.dot_general(dscat, qb, nn, preferred_element_type=jnp.float32)
    dqt = lax.dot_general(kcat.T, dscat, nn, preferred_element_type=jnp.float32)
    dq[0] = (dqt * scale).T.astype(jnp.bfloat16)
    for j, c in enumerate(places):
        part = slice(j * BLOCK, (j + 1) * BLOCK)
        acc[c, 0] += dk_part[part] * scale
        acc[c, 1] += dv_part[part]

    @pl.when(step == pl.num_programs(0) - 1)
    def _():
        count = mine.shape[0]
        mine[...] = acc[pl.ds(half[0] * count, count)]
        theirs[...] = acc[pl.ds((1 - half[0]) * count, count)].astype(jnp.bfloat16)


def local_grads(idx, bias, half, lse, delta, q, do, kv):
    steps, rows, hd = q.shape
    places = kv.shape[0]
    select = idx.shape[1]
    row = pl.BlockSpec((1, 1, rows), lambda i, *_: (i, 0, 0))
    tile = pl.BlockSpec((1, rows, hd), lambda i, *_: (i, 0, 0))

    def whole(n):
        return pl.BlockSpec(
            (n, 2, BLOCK, hd), lambda i, *_: (0, 0, 0, 0), pipeline_mode=pl.Buffered(1)
        )

    part = (places // 2, 2, BLOCK, hd)
    return pl.pallas_call(
        functools.partial(grads_kernel, 1.0 / math.sqrt(hd)),
        out_shape=(
            jax.ShapeDtypeStruct(q.shape, jnp.bfloat16),
            jax.ShapeDtypeStruct(part, jnp.float32),
            jax.ShapeDtypeStruct(part, jnp.bfloat16),
        ),
        grid_spec=pltpu.PrefetchScalarGridSpec(
            num_scalar_prefetch=3,
            grid=(steps,),
            in_specs=[row, row, tile, tile, whole(places)],
            out_specs=(tile, whole(places // 2), whole(places // 2)),
            scratch_shapes=[pltpu.VMEM((places, 2, BLOCK, hd), jnp.float32)],
        ),
        compiler_params=pltpu.CompilerParams(vmem_limit_bytes=48 << 20),
        name="grads",
    )(idx, bias, half, lse, delta, q, do, kv)


def shards(queries, keys, values, grad_out, lse, delta, block_keys):
    uly, blks = lax.axis_size("uly"), lax.axis_size("blk")
    tokens, heads, hd = queries.shape
    kvh = keys.shape[1]
    group = heads // kvh
    fold = uly // kvh
    u, slab = lax.axis_index("uly"), lax.axis_index("blk")
    slab_len = uly * tokens

    def mine_of(x):
        x = lax.dynamic_slice_in_dim(x, slab * slab_len, slab_len, 1)
        return x.reshape(kvh, fold, tokens).transpose(1, 0, 2)

    kv = jnp.stack([keys, values], 0).transpose(2, 0, 1, 3)
    q, do, kv, lse_rows, delta_rows = inbound(
        uly,
        blks,
        queries.reshape(tokens, kvh, group, hd),
        grad_out.reshape(tokens, kvh, group, hd),
        kv,
        mine_of(lse),
        mine_of(delta),
    )

    def rows_of(x):
        return x.transpose(1, 2, 0).reshape(kvh, 1, tokens * group)

    own_blocks = lax.dynamic_slice_in_dim(block_keys, slab * uly, uly, 0)
    own_blocks = lax.dynamic_index_in_dim(
        own_blocks.reshape(kvh, fold, -1), u % fold, 1, keepdims=False
    )
    own_at = jnp.where(own_blocks >= 0, own_blocks, own_blocks[:, :1])
    rel = own_at - (slab - 1) * uly
    part, home = rel // uly, rel % uly
    y, z, c = home // fold, home % fold // 2, home % 2
    idx = ((c * 2 + part) * 2 + z) * kvh + y
    bias = jnp.where(own_blocks >= 0, 0.0, OFF).astype(jnp.float32)

    dq, mine, theirs = local_grads(
        idx,
        bias,
        (u % 2).reshape(1).astype(jnp.int32),
        rows_of(lse_rows),
        rows_of(delta_rows),
        q.reshape(kvh, tokens * group, hd),
        do.reshape(kvh, tokens * group, hd),
        kv.reshape(uly * 2, 2, tokens, hd),
    )
    part = (2, 2, kvh, 2, tokens, hd)
    grad_q, home = outbound(
        uly,
        blks,
        dq.reshape(kvh, tokens, group, hd),
        mine.reshape(part),
        theirs.reshape(part),
    )
    home = home.transpose(1, 2, 0, 3)
    return grad_q.reshape(tokens, heads, hd), home[0], home[1]


def solution(mesh):
    data = P(("blk", "uly"), None, None)
    return jax.shard_map(
        shards,
        mesh=mesh,
        in_specs=(data, data, data, data, P("uly", None), P("uly", None), P()),
        out_specs=(data, data, data),
        check_vma=False,
    )
```

```python
import functools
import math

import jax
import jax.numpy as jnp
from jax import lax
from jax.experimental import pallas as pl
from jax.experimental.pallas import tpu as pltpu
from jax.sharding import PartitionSpec as P

BLOCK = 128
OFF = -1e30
MESH = pl.DeviceIdType.MESH
NT = (((1,), (1,)), ((), ()))
NN = (((1,), (0,)), ((), ()))
NEAR_FIRST = (0, 1, 7, 2, 6, 3, 5, 4)
WIDE = 4


def near_first(i):
    return jnp.where(i % 2 == 1, (i + 1) // 2, (8 - i // 2) % 8)


class Place:
    def __init__(self, uly, blks, rows):
        self.fold = uly // rows
        self.rows = rows
        self.u, self.slab = lax.axis_index("uly"), lax.axis_index("blk")
        self.y, self.r = self.u // self.fold, self.u % self.fold
        self.z, self.c = self.r // 2, self.r % 2
        self.has_before, self.has_after = self.slab > 0, self.slab < blks - 1
        self.core = self.at(self.z * 2 + 1 - self.c)
        self.other = self.at((1 - self.z) * 2 + self.c)
        self.cross = self.at((1 - self.z) * 2 + 1 - self.c)
        self.after, self.before = {"blk": self.slab + 1}, {"blk": self.slab - 1}
        x = self.slab % WIDE
        inner = self.slab >= WIDE
        self.detours = jnp.logical_and(x == 0, inner)
        self.relays = jnp.logical_and(x == WIDE - 1, inner)
        self.detoured = jnp.logical_and(x == WIDE - 1, self.slab < blks - 1)
        self.relay = {"blk": self.slab + WIDE - 1}
        self.relayed = {"blk": self.slab - WIDE + 1}
        self.relay_to = {"blk": self.slab - WIDE}
        self.relay_from = {"blk": self.slab + WIDE}

    def at(self, r):
        return {"uly": self.y * self.fold + r}

    def row(self, y):
        return {"uly": y * self.fold + self.r}

    def y_at(self, distance):
        return (self.y + distance) % self.rows

    def meet(self):
        barrier = pltpu.get_barrier_semaphore()

        def greet(device):
            pl.semaphore_signal(barrier, inc=1, device_id=device, device_id_type=MESH)

        for d in range(1, self.rows):
            greet(self.row(self.y_at(d)))
        for device in (self.core, self.other, self.cross):
            greet(device)
        count = self.rows + 2
        for there, device in (
            (self.has_after, self.after),
            (self.has_before, self.before),
            (self.detours, self.relay),
            (self.relays, self.relayed),
            (self.relays, self.relay_to),
            (self.detoured, self.relay_from),
        ):
            pl.when(there)(functools.partial(greet, device))
            count = count + there.astype(jnp.int32)
        pl.semaphore_wait(barrier, count)


def remote(src, dst, send, recv, device):
    return pltpu.make_async_remote_copy(
        src_ref=src,
        dst_ref=dst,
        send_sem=send,
        recv_sem=recv,
        device_id=device,
        device_id_type=MESH,
    )


def kernel(uly, blks, scale, idx, bias, slots, q, do, keys, vals, lse, delta,
           grad_q, home, q_parts, do_parts, dq_parts,
           kv, q_all, do_all, lse_all, delta_all, lse_rows, delta_rows, dq_all, terms,
           to_c, from_c, to_x, from_x, relay, to_z, from_z, total, to_y,
           own_s, own_d, part_q, part_do, dq_s, last_s,
           k_ss, k_rs, v_ss, v_rs, q_ss, q_rs, do_ss, do_rs, l_ss, l_rs, e_ss, e_rs,
           z_ss, z_rs, x_ss, x_rs, c_ss, c_rs,
           gq_ss, gq_rs, tc_ss, tc_rs, tx_ss, tx_rs, re_ss, re_rs, fw_ss, tz_ss, tz_rs, ty_ss, ty_rs):
    rows = keys.shape[0]
    group = lse_all.shape[0]
    wide = q_all.shape[1]
    hd = q_all.shape[2]
    select = terms.shape[0] // rows
    me = Place(uly, blks, rows)
    y, r, z, c, slab = me.y, me.r, me.z, me.c, me.slab
    has_after, has_before = me.has_after, me.has_before

    def flat(half, part, zz, t):
        return ((half * 2 + part) * 2 + zz) * rows + t

    def q_part(d):
        t = me.y_at(d)
        return pltpu.make_async_copy(q.at[:, t], q_parts.at[t], part_q.at[d])

    def do_part(d):
        t = me.y_at(d)
        return pltpu.make_async_copy(do.at[:, t], do_parts.at[t], part_do.at[d])

    def rows_of(parts, t):
        return parts.at[t].reshape(wide, hd)

    q_part(0).start()
    do_part(0).start()
    here = kv.at[flat(c, 1, z, y)]
    locals_ = [
        pltpu.make_async_copy(keys.at[y], here.at[0], own_s.at[0]),
        pltpu.make_async_copy(vals.at[y], here.at[1], own_s.at[1]),
        pltpu.make_async_copy(lse.at[slab, :, r], lse_all.at[r], own_s.at[2]),
        pltpu.make_async_copy(delta.at[slab, :, r], delta_all.at[r], own_s.at[3]),
    ]
    for copy in locals_:
        copy.start()
    me.meet()

    sends = []
    for d in NEAR_FIRST[1:]:
        t = me.y_at(d)
        sends.append(remote(keys.at[t], here.at[0], k_ss.at[d], k_rs.at[d], me.row(t)))
        sends.append(remote(vals.at[t], here.at[1], v_ss.at[d], v_rs.at[d], me.row(t)))
    for i in range(1, me.fold):
        t = (r + i) % me.fold
        sends.append(remote(lse.at[slab, :, t], lse_all.at[r], l_ss.at[i], l_rs.at[i], me.at(t)))
        sends.append(
            remote(delta.at[slab, :, t], delta_all.at[r], e_ss.at[i], e_rs.at[i], me.at(t))
        )
    for copy in sends:
        copy.start()
    for d in NEAR_FIRST[1:]:
        t = me.y_at(d)
        sends.append(remote(q.at[:, t], q_parts.at[y], q_ss.at[d], q_rs.at[d], me.row(t)))
        sends[-1].start()
        sends.append(remote(do.at[:, t], do_parts.at[y], do_ss.at[d], do_rs.at[d], me.row(t)))
        sends[-1].start()

    def place(half, part, zz, d):
        return kv.at[flat(half, part, zz, me.y_at(rows - d))]

    def from_row(d):
        there = place(c, 1, z, d)
        remote(there.at[0], there.at[0], k_ss.at[d], k_rs.at[d], me.core).wait_recv()
        remote(there.at[1], there.at[1], v_ss.at[d], v_rs.at[d], me.core).wait_recv()

    def with_other(zz, d):
        there = place(c, 1, zz, d)
        return remote(there, there, z_ss.at[d], z_rs.at[d], me.other)

    def to_after(zz, i, d):
        src, dst = place(c, 1, zz, d), place(c, 0, zz, d)
        return remote(src, dst, x_ss.at[i], x_rs.at[i], me.after)

    def from_before(zz, i, d):
        dst = place(c, 0, zz, d)
        return remote(dst, dst, x_ss.at[i], x_rs.at[i], me.before)

    def with_core(half, part, zz, i, d):
        there = place(half, part, zz, d)
        return remote(there, there, c_ss.at[i], c_rs.at[i], me.core)

    for d in NEAR_FIRST:
        if d == 0:
            locals_[0].wait()
            locals_[1].wait()
        else:
            from_row(d)
        with_other(z, d).start()
        pl.when(has_after)(lambda: to_after(z, d, d).start())
        with_core(c, 1, z, d, d).start()

    locals_[2].wait()
    locals_[3].wait()
    for i in range(1, me.fold):
        t = (r + me.fold - i) % me.fold
        remote(lse_all.at[t], lse_all.at[t], l_ss.at[i], l_rs.at[i], me.core).wait_recv()
        remote(delta_all.at[t], delta_all.at[t], e_ss.at[i], e_rs.at[i], me.core).wait_recv()
    token = lax.broadcasted_iota(jnp.int32, (BLOCK, wide), 0)
    at = lax.broadcasted_iota(jnp.int32, (BLOCK, wide), 1)
    spread = [(at == token * group + s).astype(jnp.float32) for s in range(group)]
    for rows_ref, every in ((lse_rows, lse_all), (delta_rows, delta_all)):
        rows_ref[...] = sum(
            lax.dot_general(
                every[s].reshape(rows, BLOCK),
                spread[s],
                NN,
                precision=lax.Precision.HIGHEST,
                preferred_element_type=jnp.float32,
            )
            for s in range(group)
        )
    terms[rows * select] = jnp.zeros_like(terms[rows * select])

    @pl.loop(0, rows)
    def _(i):
        d = near_first(i)
        with_other(1 - z, d).wait_recv()
        pl.when(has_after)(lambda: to_after(1 - z, rows + d, d).start())
        with_core(c, 1, 1 - z, rows + d, d).start()

        @pl.when(has_before)
        def _():
            from_before(z, d, d).wait_recv()
            with_core(c, 0, z, 2 * rows + d, d).start()

    @pl.when(has_before)
    def _():
        @pl.loop(0, rows)
        def _(i):
            d = near_first(i)
            from_before(1 - z, rows + d, d).wait_recv()
            with_core(c, 0, 1 - z, 3 * rows + d, d).start()

    @pl.when(jnp.logical_not(has_before))
    def _():
        for half in (0, 1):
            first = flat(half, 0, 0, 0)
            for i in range(2 * rows):
                kv[first + i] = jnp.zeros_like(kv[first + i])

    @pl.loop(0, rows)
    def _(d):
        for part, zz, base in ((1, z, 0), (1, 1 - z, rows)):
            with_core(1 - c, part, zz, base + d, d).wait_recv()

        @pl.when(has_before)
        def _():
            for part, zz, base in ((0, z, 2 * rows), (0, 1 - z, 3 * rows)):
                with_core(1 - c, part, zz, base + d, d).wait_recv()

    def dq_part(t, d):
        return pltpu.make_async_copy(dq_all.at[t], rows_of(dq_parts, t), dq_s.at[d])

    def dq_home(t, d):
        return remote(
            dq_parts.at[t], grad_q.at[:, y], gq_ss.at[d], gq_rs.at[d], me.row(t)
        )

    def send_dq(i):
        d = near_first(i)
        t = me.y_at(rows - d)
        dq_part(t, d).wait()

        @pl.when(d == 0)
        def _():
            pltpu.make_async_copy(dq_parts.at[t], grad_q.at[:, t], last_s.at[0]).start()

        pl.when(d > 0)(lambda: dq_home(t, d).start())

    def loads(d):
        t = me.y_at(rows - d)
        return (
            pltpu.make_async_copy(rows_of(q_parts, t), q_all.at[t], part_q.at[d]),
            pltpu.make_async_copy(rows_of(do_parts, t), do_all.at[t], part_do.at[d]),
        )

    q_part(0).wait()
    do_part(0).wait()
    for copy in loads(0):
        copy.start()

    @pl.loop(0, rows)
    def _(i):
        d = near_first(i)
        t = me.y_at(rows - d)

        @pl.when(i < rows - 1)
        def _():
            d = near_first(i + 1)
            t = me.y_at(rows - d)
            remote(q_parts.at[t], q_parts.at[t], q_ss.at[d], q_rs.at[d], me.core).wait_recv()
            remote(do_parts.at[t], do_parts.at[t], do_ss.at[d], do_rs.at[d], me.core).wait_recv()
            for copy in loads(d):
                copy.start()

        for copy in loads(d):
            copy.wait()

        places = [idx[t * select + j] for j in range(select)]
        kcat = jnp.concatenate([kv[p, 0] for p in places], 0)
        vcat = jnp.concatenate([kv[p, 1] for p in places], 0)
        qb, dob = q_all[t], do_all[t]
        s = lax.dot_general(kcat, qb, NT, preferred_element_type=jnp.float32)
        dp = lax.dot_general(vcat, dob, NT, preferred_element_type=jnp.float32)
        lse_row, delta_row = lse_rows[pl.ds(t, 1)], delta_rows[pl.ds(t, 1)]
        probs, dscores = [], []
        for j in range(select):
            part = slice(j * BLOCK, (j + 1) * BLOCK)
            p = jnp.exp(s[part] * scale - (lse_row - bias[t * select + j]))
            if j == 0:
                key_at = lax.broadcasted_iota(jnp.int32, (BLOCK, wide), 0)
                query_at = lax.broadcasted_iota(jnp.int32, (BLOCK, wide), 1) // group
                p = jnp.where(key_at <= query_at, p, 0.0)
            ds = p * (dp[part] - delta_row)
            probs.append(p.astype(jnp.bfloat16))
            dscores.append(ds.astype(jnp.bfloat16))
        pcat = jnp.concatenate(probs, 0)
        dscat = jnp.concatenate(dscores, 0)
        dqt = lax.dot_general(kcat.T, dscat, NN, preferred_element_type=jnp.float32)
        dq_all[t] = (dqt * scale).T.astype(jnp.bfloat16)
        dq_part(t, d).start()
        dk_part = lax.dot_general(dscat, qb, NN, preferred_element_type=jnp.float32) * scale
        dv_part = lax.dot_general(pcat, dob, NN, preferred_element_type=jnp.float32)
        for j in range(select):
            part = slice(j * BLOCK, (j + 1) * BLOCK)
            terms[t * select + j, 0] = dk_part[part]
            terms[t * select + j, 1] = dv_part[part]
        pl.when(i > 0)(lambda: send_dq(i - 1))

    send_dq(rows - 1)

    def gathered(half, part, zz, t):
        at_ = flat(half, part, zz, t) * rows
        x = terms[slots[at_]]
        for b in range(1, rows):
            x = x + terms[slots[at_ + b]]
        return x

    def core(part, zz, order, d):
        t = me.y_at(d)
        i = (part * 2 + order) * rows + d
        place_ = (part * 2 + zz) * rows + t
        return remote(to_c.at[place_], from_c.at[place_], tc_ss.at[i], tc_rs.at[i], me.core)

    def before(zz, order, d):
        t, i = me.y_at(d), order * rows + d
        return remote(to_x.at[zz, t], from_x.at[zz, t], tx_ss.at[i], tx_rs.at[i], me.before)

    def detour(d):
        t = me.y_at(d)
        return remote(to_x.at[z, t], relay.at[t], tx_ss.at[rows + d], re_rs.at[d], me.relay)

    def forward(d):
        t = me.y_at(d)
        return remote(relay.at[t], from_x.at[z, t], fw_ss.at[d], tx_rs.at[rows + d], me.relay_to)

    def relay_in(d):
        t = me.y_at(d)
        return remote(relay.at[t], relay.at[t], re_ss.at[d], re_rs.at[d], me.relayed)

    def other(d):
        t = me.y_at(d)
        return remote(to_z.at[t], from_z.at[t], tz_ss.at[d], tz_rs.at[d], me.other)

    def back(d):
        t = me.y_at(d)
        return remote(to_y.at[t], home.at[y], ty_ss.at[d], ty_rs.at[d], me.row(t))

    direct = jnp.logical_and(has_before, jnp.logical_not(me.detours))
    ways = ((1 - z, 0), (z, 1))
    for part in (0, 1):
        for zz, order in ways:

            @pl.loop(0, rows)
            def _(d):
                t = me.y_at(d)
                to_c[(part * 2 + zz) * rows + t] = gathered(1 - c, part, zz, t).astype(jnp.bfloat16)
                core(part, zz, order, d).start()

    for zz, order in ways:

        @pl.loop(0, rows)
        def _(d):
            t = me.y_at(d)
            core(0, zz, order, d).wait_recv()

            @pl.when(has_before)
            def _():
                x = gathered(c, 0, zz, t) + from_c[zz * rows + t]
                to_x[zz, t] = x.astype(jnp.bfloat16)

            if order == 0:
                pl.when(has_before)(lambda: before(zz, 0, d).start())
            else:
                pl.when(direct)(lambda: before(zz, 1, d).start())
                pl.when(me.detours)(lambda: detour(d).start())

    def summed(zz, order, d, store):
        t = me.y_at(d)
        core(1, zz, order, d).wait_recv()
        x = gathered(c, 1, zz, t) + from_c[(2 + zz) * rows + t]

        @pl.when(has_after)
        def _():
            before(zz, order, d).wait_recv()
            store(t, x + from_x[zz, t])

        pl.when(jnp.logical_not(has_after))(lambda: store(t, x))

    @pl.loop(0, rows)
    def _(d):
        def store(t, x):
            to_z[t] = x.astype(jnp.bfloat16)

        summed(1 - z, 0, d, store)
        other(d).start()

        @pl.when(me.relays)
        def _():
            relay_in(d).wait_recv()
            forward(d).start()

    @pl.loop(0, rows)
    def _(d):
        def store(t, x):
            total[...] = x

        summed(z, 1, d, store)
        other(d).wait_recv()
        t = me.y_at(d)
        to_y[t] = (total[...] + from_z[t]).astype(jnp.bfloat16)
        pl.when(d > 0)(lambda: back(d).start())

    last = pltpu.make_async_copy(to_y.at[y], home.at[y], last_s.at[1])
    last.start()

    for copy in sends:
        copy.wait_send()

    @pl.loop(0, rows)
    def _(d):
        with_other(z, d).wait_send()
        for zz, base in ((z, 0), (1 - z, rows)):
            with_core(c, 1, zz, base + d, d).wait_send()
            pl.when(has_after)(lambda: to_after(zz, base + d, d).wait_send())
            pl.when(has_before)(lambda: with_core(c, 0, zz, 2 * rows + base + d, d).wait_send())
        for part in (0, 1):
            for zz, order in ways:
                core(part, zz, order, d).wait_send()
        for zz, order in ways:
            pl.when(has_before)(lambda: before(zz, order, d).wait_send())
        other(d).wait_send()
        pl.when(me.relays)(lambda: forward(d).wait_send())

    @pl.loop(1, rows)
    def _(d):
        t = me.y_at(rows - d)
        dq_home(t, d).wait_send()
        back(d).wait_send()
        far = me.y_at(d)
        remote(
            dq_parts.at[far], grad_q.at[:, far], gq_ss.at[d], gq_rs.at[d], me.core
        ).wait_recv()
        remote(to_y.at[t], home.at[t], ty_ss.at[d], ty_rs.at[d], me.core).wait_recv()

    pltpu.make_async_copy(dq_parts.at[y], grad_q.at[:, y], last_s.at[0]).wait()
    last.wait()


def shards(queries, keys, values, grad_out, lse, delta, block_keys):
    uly, blks = lax.axis_size("uly"), lax.axis_size("blk")
    tokens, heads, hd = queries.shape
    kvh = keys.shape[1]
    group, fold = heads // kvh, uly // kvh
    wide = tokens * group
    select = block_keys.shape[1]
    u, slab = lax.axis_index("uly"), lax.axis_index("blk")

    own_blocks = lax.dynamic_slice_in_dim(block_keys, slab * uly, uly, 0)
    own_blocks = lax.dynamic_index_in_dim(
        own_blocks.reshape(kvh, fold, -1), u % fold, 1, keepdims=False
    )
    valid = own_blocks >= 0
    own_at = jnp.where(valid, own_blocks, own_blocks[:, :1])
    rel = own_at - (slab - 1) * uly
    part, at = rel // uly, rel % uly
    y, z, c = at // fold, at % fold // 2, at % 2
    idx = ((c * 2 + part) * 2 + z) * kvh + y
    bias = jnp.where(valid, 0.0, OFF).astype(jnp.float32)
    count = kvh * select
    slot = jnp.arange(count, dtype=jnp.int32).reshape(kvh, select)
    listed = (idx == jnp.arange(2 * uly, dtype=jnp.int32)[:, None, None]) & valid
    slots = count + jnp.where(listed, slot - count, 0).sum(2, dtype=jnp.int32)

    low, f32 = jnp.bfloat16, jnp.float32
    hbm, smem = pl.BlockSpec(memory_space=pltpu.HBM), pl.BlockSpec(memory_space=pltpu.SMEM)
    piece = (2, tokens, hd)
    parts = jax.ShapeDtypeStruct((kvh, tokens, group, hd), low)
    dma = pltpu.SemaphoreType.DMA
    by_row = (blks, kvh, fold, 1, tokens)
    grad_q, home, *_ = pl.pallas_call(
        functools.partial(kernel, uly, blks, 1.0 / math.sqrt(hd)),
        out_shape=(
            jax.ShapeDtypeStruct((tokens, kvh, group, hd), low),
            jax.ShapeDtypeStruct((kvh,) + piece, low),
            parts,
            parts,
            parts,
        ),
        in_specs=[smem] * 3 + [hbm] * 6,
        out_specs=(hbm,) * 5,
        scratch_shapes=[
            pltpu.VMEM((2 * uly,) + piece, low),
            pltpu.VMEM((kvh, wide, hd), low),
            pltpu.VMEM((kvh, wide, hd), low),
            pltpu.VMEM((group, kvh, 1, tokens), f32),
            pltpu.VMEM((group, kvh, 1, tokens), f32),
            pltpu.VMEM((kvh, wide), f32),
            pltpu.VMEM((kvh, wide), f32),
            pltpu.VMEM((kvh, wide, hd), low),
            pltpu.VMEM((count + 1,) + piece, f32),
            pltpu.VMEM((uly,) + piece, low),
            pltpu.VMEM((uly,) + piece, low),
            pltpu.VMEM((2, kvh) + piece, low),
            pltpu.VMEM((2, kvh) + piece, low),
            pltpu.VMEM((kvh,) + piece, low),
            pltpu.VMEM((kvh,) + piece, low),
            pltpu.VMEM((kvh,) + piece, low),
            pltpu.VMEM(piece, f32),
            pltpu.VMEM((kvh,) + piece, low),
            dma((6,)),
            dma((6,)),
            dma((kvh,)),
            dma((kvh,)),
            dma((kvh,)),
            dma((2,)),
        ]
        + [dma((kvh,))] * 8
        + [dma((fold,))] * 4
        + [dma((kvh,))] * 2
        + [dma((2 * kvh,))] * 2
        + [dma((4 * kvh,))] * 2
        + [dma((kvh,))] * 2
        + [dma((4 * kvh,))] * 2
        + [dma((2 * kvh,))] * 2
        + [dma((kvh,))] * 7,
        compiler_params=pltpu.CompilerParams(
            collective_id=0, has_side_effects=True, vmem_limit_bytes=56 << 20
        ),
        name="grads",
    )(
        idx.reshape(-1),
        bias.reshape(-1),
        slots.reshape(-1),
        queries.reshape(tokens, kvh, group, hd),
        grad_out.reshape(tokens, kvh, group, hd),
        keys.transpose(1, 0, 2),
        values.transpose(1, 0, 2),
        lse.reshape(by_row),
        delta.reshape(by_row),
    )
    home = home.transpose(1, 2, 0, 3)
    return grad_q.reshape(tokens, heads, hd), home[0], home[1]


def solution(mesh):
    data = P(("blk", "uly"), None, None)
    return jax.shard_map(
        shards,
        mesh=mesh,
        in_specs=(data, data, data, data, P("uly", None), P("uly", None), P()),
        out_specs=(data, data, data),
        check_vma=False,
    )
```

```python
import functools
import math

import jax
import jax.numpy as jnp
from jax import lax
from jax.experimental import pallas as pl
from jax.experimental.pallas import tpu as pltpu
from jax.sharding import PartitionSpec as P

BLOCK = 128
OFF = -1e30
MESH = pl.DeviceIdType.MESH
NT = (((1,), (1,)), ((), ()))
NN = (((1,), (0,)), ((), ()))
NEAR_FIRST = (0, 1, 7, 2, 6, 3, 5, 4)
WIDE = 4


def near_first(i):
    return jnp.where(i % 2 == 1, (i + 1) // 2, (8 - i // 2) % 8)


class Place:
    def __init__(self, uly, blks, rows):
        self.fold = uly // rows
        self.rows = rows
        self.u, self.slab = lax.axis_index("uly"), lax.axis_index("blk")
        self.y, self.r = self.u // self.fold, self.u % self.fold
        self.z, self.c = self.r // 2, self.r % 2
        self.has_before, self.has_after = self.slab > 0, self.slab < blks - 1
        self.core = self.at(self.z * 2 + 1 - self.c)
        self.other = self.at((1 - self.z) * 2 + self.c)
        self.cross = self.at((1 - self.z) * 2 + 1 - self.c)
        self.after, self.before = {"blk": self.slab + 1}, {"blk": self.slab - 1}
        self.x = self.slab % WIDE
        run, runs = self.slab // WIDE, blks // WIDE
        self.ends = jnp.logical_and(self.x == WIDE - 1, run < runs - 1)
        self.starts = jnp.logical_and(self.x == 0, run > 0)
        self.carries = jnp.logical_and(self.x < WIDE - 1, run < runs - 1)
        self.returns = jnp.logical_and(self.x > 0, run > 0)
        self.blks = blks

    def column(self, x):
        return {"blk": self.slab - self.x + x}

    def at(self, r):
        return {"uly": self.y * self.fold + r}

    def row(self, y):
        return {"uly": y * self.fold + self.r}

    def y_at(self, distance):
        return (self.y + distance) % self.rows

    def meet(self):
        barrier = pltpu.get_barrier_semaphore()

        def greet(device):
            pl.semaphore_signal(barrier, inc=1, device_id=device, device_id_type=MESH)

        for d in range(1, self.rows):
            greet(self.row(self.y_at(d)))
        for device in (self.core, self.other, self.cross):
            greet(device)
        count = self.rows + 2
        for k in range(1, WIDE + 1):
            for there, device in (
                (self.slab + k < self.blks, {"blk": self.slab + k}),
                (self.slab >= k, {"blk": self.slab - k}),
            ):
                pl.when(there)(functools.partial(greet, device))
                count = count + there.astype(jnp.int32)
        pl.semaphore_wait(barrier, count)


def remote(src, dst, send, recv, device):
    return pltpu.make_async_remote_copy(
        src_ref=src,
        dst_ref=dst,
        send_sem=send,
        recv_sem=recv,
        device_id=device,
        device_id_type=MESH,
    )


def kernel(uly, blks, scale, idx, bias, slots, q, do, keys, vals, lse, delta,
           grad_q, home_k, home_v, q_parts, do_parts, dq_parts,
           kv, q_all, do_all, lse_all, delta_all, lse_rows, delta_rows, dq_all, terms,
           to_c, from_c, to_x, from_x, carried, relay, to_z, from_z, total, to_y,
           own_s, own_d, part_q, part_do, dq_s, last_s,
           k_ss, k_rs, v_ss, v_rs, q_ss, q_rs, do_ss, do_rs, l_ss, l_rs, e_ss, e_rs,
           z_ss, z_rs, x_ss, x_rs, c_ss, c_rs,
           gq_ss, gq_rs, tc_ss, tc_rs, tx_ss, tx_rs, re_ss, re_rs, fw_ss, tz_ss, tz_rs, ty_ss, ty_rs, tv_ss, tv_rs, ca_rs, cf_ss):
    rows = keys.shape[0]
    group = lse_all.shape[0]
    wide = q_all.shape[1]
    hd = q_all.shape[2]
    select = terms.shape[0] // rows
    me = Place(uly, blks, rows)
    y, r, z, c, slab = me.y, me.r, me.z, me.c, me.slab
    has_after, has_before = me.has_after, me.has_before

    def flat(half, part, zz, t):
        return ((half * 2 + part) * 2 + zz) * rows + t

    def q_part(d):
        t = me.y_at(d)
        return pltpu.make_async_copy(q.at[:, t], q_parts.at[t], part_q.at[d])

    def do_part(d):
        t = me.y_at(d)
        return pltpu.make_async_copy(do.at[:, t], do_parts.at[t], part_do.at[d])

    def rows_of(parts, t):
        return parts.at[t].reshape(wide, hd)

    q_part(0).start()
    do_part(0).start()
    here = kv.at[flat(c, 1, z, y)]
    locals_ = [
        pltpu.make_async_copy(keys.at[y], here.at[0], own_s.at[0]),
        pltpu.make_async_copy(vals.at[y], here.at[1], own_s.at[1]),
        pltpu.make_async_copy(lse.at[slab, :, r], lse_all.at[r], own_s.at[2]),
        pltpu.make_async_copy(delta.at[slab, :, r], delta_all.at[r], own_s.at[3]),
    ]
    for copy in locals_:
        copy.start()
    me.meet()

    sends = []
    for d in NEAR_FIRST[1:]:
        t = me.y_at(d)
        sends.append(remote(keys.at[t], here.at[0], k_ss.at[d], k_rs.at[d], me.row(t)))
        sends.append(remote(vals.at[t], here.at[1], v_ss.at[d], v_rs.at[d], me.row(t)))
    for i in range(1, me.fold):
        t = (r + i) % me.fold
        sends.append(remote(lse.at[slab, :, t], lse_all.at[r], l_ss.at[i], l_rs.at[i], me.at(t)))
        sends.append(
            remote(delta.at[slab, :, t], delta_all.at[r], e_ss.at[i], e_rs.at[i], me.at(t))
        )
    for copy in sends:
        copy.start()

    def send_queries(distances):
        for d in distances:
            t = me.y_at(d)
            for copy in (
                remote(q.at[:, t], q_parts.at[y], q_ss.at[d], q_rs.at[d], me.row(t)),
                remote(do.at[:, t], do_parts.at[y], do_ss.at[d], do_rs.at[d], me.row(t)),
            ):
                copy.start()
                sends.append(copy)

    send_queries((1, 7, 2))

    def place(half, part, zz, d):
        return kv.at[flat(half, part, zz, me.y_at(rows - d))]

    def from_row(d):
        there = place(c, 1, z, d)
        remote(there.at[0], there.at[0], k_ss.at[d], k_rs.at[d], me.core).wait_recv()
        remote(there.at[1], there.at[1], v_ss.at[d], v_rs.at[d], me.core).wait_recv()

    def with_other(zz, d):
        there = place(c, 1, zz, d)
        return remote(there, there, z_ss.at[d], z_rs.at[d], me.other)

    def to_after(zz, i, d):
        src, dst = place(c, 1, zz, d), place(c, 0, zz, d)
        return remote(src, dst, x_ss.at[i], x_rs.at[i], me.after)

    def pass_on(zz, order, d):
        i = order * rows + d
        straight = jnp.logical_or(jnp.logical_not(me.ends), d % WIDE == WIDE - 1)
        pl.when(jnp.logical_and(has_after, straight))(lambda: to_after(zz, i, d).start())

        @pl.when(jnp.logical_not(straight))
        def _():
            k = order * 2 + d // WIDE
            remote(
                place(c, 1, zz, d), carried.at[k], x_ss.at[i], ca_rs.at[k], me.column(d % WIDE)
            ).start()

    def carry(zz, order, k):
        d = me.x + k * WIDE
        at_ = order * 2 + k
        dst = place(c, 0, zz, d)
        return remote(
            carried.at[at_], dst, cf_ss.at[at_], x_rs.at[order * rows + d], me.column(WIDE)
        )

    def carry_on(zz, order):
        @pl.when(me.carries)
        def _():
            for k in (0, 1):
                at_ = order * 2 + k
                remote(
                    carried.at[at_], carried.at[at_], cf_ss.at[at_], ca_rs.at[at_], me.core
                ).wait_recv()
                carry(zz, order, k).start()

    def from_before(zz, i, d):
        dst = place(c, 0, zz, d)
        return remote(dst, dst, x_ss.at[i], x_rs.at[i], me.before)

    def with_core(half, part, zz, i, d):
        there = place(half, part, zz, d)
        return remote(there, there, c_ss.at[i], c_rs.at[i], me.core)

    for d in NEAR_FIRST:
        if d == 0:
            locals_[0].wait()
            locals_[1].wait()
        else:
            from_row(d)
        with_other(z, d).start()
        pass_on(z, 0, jnp.int32(d))
        with_core(c, 1, z, d, d).start()

    send_queries((6, 3))
    carry_on(z, 0)

    locals_[2].wait()
    locals_[3].wait()
    for i in range(1, me.fold):
        t = (r + me.fold - i) % me.fold
        remote(lse_all.at[t], lse_all.at[t], l_ss.at[i], l_rs.at[i], me.core).wait_recv()
        remote(delta_all.at[t], delta_all.at[t], e_ss.at[i], e_rs.at[i], me.core).wait_recv()
    token = lax.broadcasted_iota(jnp.int32, (BLOCK, wide), 0)
    at = lax.broadcasted_iota(jnp.int32, (BLOCK, wide), 1)
    spread = [(at == token * group + s).astype(jnp.float32) for s in range(group)]
    for rows_ref, every in ((lse_rows, lse_all), (delta_rows, delta_all)):
        rows_ref[...] = sum(
            lax.dot_general(
                every[s].reshape(rows, BLOCK),
                spread[s],
                NN,
                precision=lax.Precision.HIGHEST,
                preferred_element_type=jnp.float32,
            )
            for s in range(group)
        )
    terms[rows * select] = jnp.zeros_like(terms[rows * select])

    def hand_on(i):
        d = near_first(i)
        with_other(1 - z, d).wait_recv()
        pass_on(1 - z, 1, d)
        with_core(c, 1, 1 - z, rows + d, d).start()

        @pl.when(has_before)
        def _():
            from_before(z, d, d).wait_recv()
            with_core(c, 0, z, 2 * rows + d, d).start()

    pl.loop(0, rows // 2)(hand_on)
    send_queries((5, 4))
    pl.loop(rows // 2, rows)(hand_on)
    carry_on(1 - z, 1)

    @pl.when(has_before)
    def _():
        @pl.loop(0, rows)
        def _(i):
            d = near_first(i)
            from_before(1 - z, rows + d, d).wait_recv()
            with_core(c, 0, 1 - z, 3 * rows + d, d).start()

    @pl.when(jnp.logical_not(has_before))
    def _():
        for half in (0, 1):
            first = flat(half, 0, 0, 0)
            for i in range(2 * rows):
                kv[first + i] = jnp.zeros_like(kv[first + i])

    @pl.loop(0, rows)
    def _(d):
        for part, zz, base in ((1, z, 0), (1, 1 - z, rows)):
            with_core(1 - c, part, zz, base + d, d).wait_recv()

        @pl.when(has_before)
        def _():
            for part, zz, base in ((0, z, 2 * rows), (0, 1 - z, 3 * rows)):
                with_core(1 - c, part, zz, base + d, d).wait_recv()

    def dq_part(t, d):
        return pltpu.make_async_copy(dq_all.at[t], rows_of(dq_parts, t), dq_s.at[d])

    def dq_home(t, d):
        return remote(
            dq_parts.at[t], grad_q.at[:, y], gq_ss.at[d], gq_rs.at[d], me.row(t)
        )

    def send_dq(i):
        d = near_first(i)
        t = me.y_at(rows - d)
        dq_part(t, d).wait()

        @pl.when(d == 0)
        def _():
            pltpu.make_async_copy(dq_parts.at[t], grad_q.at[:, t], last_s.at[0]).start()

        pl.when(d > 0)(lambda: dq_home(t, d).start())

    def loads(d):
        t = me.y_at(rows - d)
        return (
            pltpu.make_async_copy(rows_of(q_parts, t), q_all.at[t], part_q.at[d]),
            pltpu.make_async_copy(rows_of(do_parts, t), do_all.at[t], part_do.at[d]),
        )

    q_part(0).wait()
    do_part(0).wait()
    for copy in loads(0):
        copy.start()

    @pl.loop(0, rows)
    def _(i):
        d = near_first(i)
        t = me.y_at(rows - d)

        @pl.when(i < rows - 1)
        def _():
            d = near_first(i + 1)
            t = me.y_at(rows - d)
            remote(q_parts.at[t], q_parts.at[t], q_ss.at[d], q_rs.at[d], me.core).wait_recv()
            remote(do_parts.at[t], do_parts.at[t], do_ss.at[d], do_rs.at[d], me.core).wait_recv()
            for copy in loads(d):
                copy.start()

        for copy in loads(d):
            copy.wait()

        places = [idx[t * select + j] for j in range(select)]
        kcat = jnp.concatenate([kv[p, 0] for p in places], 0)
        vcat = jnp.concatenate([kv[p, 1] for p in places], 0)
        qb, dob = q_all[t], do_all[t]
        s = lax.dot_general(kcat, qb, NT, preferred_element_type=jnp.float32)
        dp = lax.dot_general(vcat, dob, NT, preferred_element_type=jnp.float32)
        lse_row, delta_row = lse_rows[pl.ds(t, 1)], delta_rows[pl.ds(t, 1)]
        probs, dscores = [], []
        for j in range(select):
            part = slice(j * BLOCK, (j + 1) * BLOCK)
            p = jnp.exp(s[part] * scale - (lse_row - bias[t * select + j]))
            if j == 0:
                key_at = lax.broadcasted_iota(jnp.int32, (BLOCK, wide), 0)
                query_at = lax.broadcasted_iota(jnp.int32, (BLOCK, wide), 1) // group
                p = jnp.where(key_at <= query_at, p, 0.0)
            ds = p * (dp[part] - delta_row)
            probs.append(p.astype(jnp.bfloat16))
            dscores.append(ds.astype(jnp.bfloat16))
        pcat = jnp.concatenate(probs, 0)
        dscat = jnp.concatenate(dscores, 0)
        dqt = lax.dot_general(kcat.T, dscat, NN, preferred_element_type=jnp.float32)
        dq_all[t] = (dqt * scale).T.astype(jnp.bfloat16)
        dq_part(t, d).start()
        dk_part = lax.dot_general(dscat, qb, NN, preferred_element_type=jnp.float32) * scale
        dv_part = lax.dot_general(pcat, dob, NN, preferred_element_type=jnp.float32)
        for j in range(select):
            part = slice(j * BLOCK, (j + 1) * BLOCK)
            terms[t * select + j, 0] = dk_part[part]
            terms[t * select + j, 1] = dv_part[part]
        pl.when(i > 0)(lambda: send_dq(i - 1))

    send_dq(rows - 1)

    def gathered(half, part, zz, t):
        at_ = flat(half, part, zz, t) * rows
        x = terms[slots[at_]]
        for b in range(1, rows):
            x = x + terms[slots[at_ + b]]
        return x

    def core(part, zz, order, d):
        t = me.y_at(d)
        i = (part * 2 + order) * rows + d
        place_ = (part * 2 + zz) * rows + t
        return remote(to_c.at[place_], from_c.at[place_], tc_ss.at[i], tc_rs.at[i], me.core)

    def before(zz, order, d):
        t, i = me.y_at(d), order * rows + d
        return remote(to_x.at[zz, t], from_x.at[zz, t], tx_ss.at[i], tx_rs.at[i], me.before)

    def detour(zz, order, d):
        t, k = me.y_at(d), order * 2 + d // WIDE
        return remote(
            to_x.at[zz, t], relay.at[k], tx_ss.at[order * rows + d], re_rs.at[k], me.column(d % WIDE)
        )

    def forward(zz, order, k):
        d = me.x + k * WIDE
        at_ = order * 2 + k
        return remote(
            relay.at[at_],
            from_x.at[zz, me.y_at(d)],
            fw_ss.at[at_],
            tx_rs.at[order * rows + d],
            me.column(-1),
        )

    def relay_in(k):
        return remote(relay.at[k], relay.at[k], re_ss.at[k], re_rs.at[k], me.core)

    def other(d):
        t = me.y_at(d)
        return remote(to_z.at[t], from_z.at[t], tz_ss.at[d], tz_rs.at[d], me.other)

    def back(d):
        t = me.y_at(d)
        return (
            remote(to_y.at[t, 0], home_k.at[y], ty_ss.at[d], ty_rs.at[d], me.row(t)),
            remote(to_y.at[t, 1], home_v.at[y], tv_ss.at[d], tv_rs.at[d], me.row(t)),
        )

    def start_back(d):
        for copy in back(d):
            copy.start()

    direct = jnp.logical_and(has_before, jnp.logical_not(me.starts))

    def offer(part, zz, order, d):
        t = me.y_at(d)
        to_c[(part * 2 + zz) * rows + t] = gathered(1 - c, part, zz, t).astype(jnp.bfloat16)
        core(part, zz, order, d).start()

    def collect(zz, order, d):
        t = me.y_at(d)
        core(0, zz, order, d).wait_recv()
        x = gathered(c, 0, zz, t) + from_c[zz * rows + t]
        to_x[zz, t] = x.astype(jnp.bfloat16)

    ways = ((1 - z, 0), (z, 1))

    @pl.loop(0, rows)
    def _(d):
        offer(0, 1 - z, 0, d)

        @pl.when(jnp.logical_not(direct))
        def _():
            offer(0, z, 1, d)

    @pl.loop(0, rows)
    def _(d):
        @pl.when(has_before)
        def _():
            collect(1 - z, 0, d)

        straight = jnp.logical_or(direct, jnp.logical_and(me.starts, d % WIDE == 0))
        pl.when(straight)(lambda: before(1 - z, 0, d).start())

        @pl.when(me.starts)
        def _():
            pl.when(d % WIDE > 0)(lambda: detour(1 - z, 0, d).start())
            collect(z, 1, d)
            pl.when(d % WIDE == 0)(lambda: before(z, 1, d).start())
            pl.when(d % WIDE > 0)(lambda: detour(z, 1, d).start())

    @pl.when(me.returns)
    def _():
        for zz, order in ways:
            for k in (0, 1):
                relay_in(order * 2 + k).wait_recv()
                forward(zz, order, k).start()

    @pl.when(direct)
    def _():
        @pl.loop(0, rows)
        def _(d):
            offer(0, z, 1, d)

    @pl.loop(0, rows)
    def _(d):
        @pl.when(direct)
        def _():
            collect(z, 1, d)
            before(z, 1, d).start()

        offer(1, 1 - z, 0, d)

    @pl.when(jnp.logical_not(has_before))
    def _():
        @pl.loop(0, rows)
        def _(d):
            core(0, 1 - z, 0, d).wait_recv()
            core(0, z, 1, d).wait_recv()

    def summed(zz, order, d, store):
        t = me.y_at(d)
        core(1, zz, order, d).wait_recv()
        x = gathered(c, 1, zz, t) + from_c[(2 + zz) * rows + t]

        @pl.when(has_after)
        def _():
            before(zz, order, d).wait_recv()
            store(t, x + from_x[zz, t])

        pl.when(jnp.logical_not(has_after))(lambda: store(t, x))

    @pl.loop(0, rows)
    def _(d):
        def store(t, x):
            to_z[t] = x.astype(jnp.bfloat16)

        offer(1, z, 1, d)
        summed(1 - z, 0, d, store)
        other(d).start()

    @pl.loop(0, rows)
    def _(d):
        def store(t, x):
            total[...] = x

        summed(z, 1, d, store)
        other(d).wait_recv()
        t = me.y_at(d)
        to_y[t] = (total[...] + from_z[t]).astype(jnp.bfloat16)
        pl.when(d > 0)(lambda: start_back(d))

    last = (
        pltpu.make_async_copy(to_y.at[y, 0], home_k.at[y], last_s.at[1]),
        pltpu.make_async_copy(to_y.at[y, 1], home_v.at[y], last_s.at[2]),
    )
    for copy in last:
        copy.start()

    for copy in sends:
        copy.wait_send()

    @pl.loop(0, rows)
    def _(d):
        with_other(z, d).wait_send()
        for zz, base in ((z, 0), (1 - z, rows)):
            with_core(c, 1, zz, base + d, d).wait_send()
            pl.when(has_after)(lambda: to_after(zz, base + d, d).wait_send())
            pl.when(has_before)(lambda: with_core(c, 0, zz, 2 * rows + base + d, d).wait_send())
        for part in (0, 1):
            for zz, order in ways:
                core(part, zz, order, d).wait_send()
        for zz, order in ways:
            pl.when(has_before)(lambda: before(zz, order, d).wait_send())
        other(d).wait_send()

    for k in (0, 1):
        for order, zz in ((0, z), (1, 1 - z)):
            pl.when(me.carries)(lambda: carry(zz, order, k).wait_send())
            pl.when(me.returns)(lambda: forward(zz, order, k).wait_send())

    @pl.loop(1, rows)
    def _(d):
        t = me.y_at(rows - d)
        dq_home(t, d).wait_send()
        for copy in back(d):
            copy.wait_send()
        far = me.y_at(d)
        remote(
            dq_parts.at[far], grad_q.at[:, far], gq_ss.at[d], gq_rs.at[d], me.core
        ).wait_recv()
        remote(home_k.at[t], home_k.at[t], ty_ss.at[d], ty_rs.at[d], me.core).wait_recv()
        remote(home_v.at[t], home_v.at[t], tv_ss.at[d], tv_rs.at[d], me.core).wait_recv()

    pltpu.make_async_copy(dq_parts.at[y], grad_q.at[:, y], last_s.at[0]).wait()
    for copy in last:
        copy.wait()


def shards(queries, keys, values, grad_out, lse, delta, block_keys):
    uly, blks = lax.axis_size("uly"), lax.axis_size("blk")
    tokens, heads, hd = queries.shape
    kvh = keys.shape[1]
    group, fold = heads // kvh, uly // kvh
    wide = tokens * group
    select = block_keys.shape[1]
    u, slab = lax.axis_index("uly"), lax.axis_index("blk")

    own_blocks = lax.dynamic_slice_in_dim(block_keys, slab * uly, uly, 0)
    own_blocks = lax.dynamic_index_in_dim(
        own_blocks.reshape(kvh, fold, -1), u % fold, 1, keepdims=False
    )
    valid = own_blocks >= 0
    own_at = jnp.where(valid, own_blocks, own_blocks[:, :1])
    rel = own_at - (slab - 1) * uly
    part, at = rel // uly, rel % uly
    y, z, c = at // fold, at % fold // 2, at % 2
    idx = ((c * 2 + part) * 2 + z) * kvh + y
    bias = jnp.where(valid, 0.0, OFF).astype(jnp.float32)
    count = kvh * select
    slot = jnp.arange(count, dtype=jnp.int32).reshape(kvh, select)
    listed = (idx == jnp.arange(2 * uly, dtype=jnp.int32)[:, None, None]) & valid
    slots = count + jnp.where(listed, slot - count, 0).sum(2, dtype=jnp.int32)

    low, f32 = jnp.bfloat16, jnp.float32
    hbm, smem = pl.BlockSpec(memory_space=pltpu.HBM), pl.BlockSpec(memory_space=pltpu.SMEM)
    piece = (2, tokens, hd)
    parts = jax.ShapeDtypeStruct((kvh, tokens, group, hd), low)
    dma = pltpu.SemaphoreType.DMA
    by_row = (blks, kvh, fold, 1, tokens)
    grad_q, home_k, home_v, *_ = pl.pallas_call(
        functools.partial(kernel, uly, blks, 1.0 / math.sqrt(hd)),
        out_shape=(
            jax.ShapeDtypeStruct((tokens, kvh, group, hd), low),
            jax.ShapeDtypeStruct((kvh,) + piece[1:], low),
            jax.ShapeDtypeStruct((kvh,) + piece[1:], low),
            parts,
            parts,
            parts,
        ),
        in_specs=[smem] * 3 + [hbm] * 6,
        out_specs=(hbm,) * 6,
        scratch_shapes=[
            pltpu.VMEM((2 * uly,) + piece, low),
            pltpu.VMEM((kvh, wide, hd), low),
            pltpu.VMEM((kvh, wide, hd), low),
            pltpu.VMEM((group, kvh, 1, tokens), f32),
            pltpu.VMEM((group, kvh, 1, tokens), f32),
            pltpu.VMEM((kvh, wide), f32),
            pltpu.VMEM((kvh, wide), f32),
            pltpu.VMEM((kvh, wide, hd), low),
            pltpu.VMEM((count + 1,) + piece, f32),
            pltpu.VMEM((uly,) + piece, low),
            pltpu.VMEM((uly,) + piece, low),
            pltpu.VMEM((2, kvh) + piece, low),
            pltpu.VMEM((2, kvh) + piece, low),
            pltpu.VMEM((4,) + piece, low),
            pltpu.VMEM((4,) + piece, low),
            pltpu.VMEM((kvh,) + piece, low),
            pltpu.VMEM((kvh,) + piece, low),
            pltpu.VMEM(piece, f32),
            pltpu.VMEM((kvh,) + piece, low),
            dma((6,)),
            dma((6,)),
            dma((kvh,)),
            dma((kvh,)),
            dma((kvh,)),
            dma((3,)),
        ]
        + [dma((kvh,))] * 8
        + [dma((fold,))] * 4
        + [dma((kvh,))] * 2
        + [dma((2 * kvh,))] * 2
        + [dma((4 * kvh,))] * 2
        + [dma((kvh,))] * 2
        + [dma((4 * kvh,))] * 2
        + [dma((2 * kvh,))] * 2
        + [dma((kvh,))] * 11,
        compiler_params=pltpu.CompilerParams(
            collective_id=0, has_side_effects=True, vmem_limit_bytes=56 << 20
        ),
        name="grads",
    )(
        idx.reshape(-1),
        bias.reshape(-1),
        slots.reshape(-1),
        queries.reshape(tokens, kvh, group, hd),
        grad_out.reshape(tokens, kvh, group, hd),
        keys.transpose(1, 0, 2),
        values.transpose(1, 0, 2),
        lse.reshape(by_row),
        delta.reshape(by_row),
    )
    return (
        grad_q.reshape(tokens, heads, hd),
        home_k.transpose(1, 0, 2),
        home_v.transpose(1, 0, 2),
    )


def solution(mesh):
    data = P(("blk", "uly"), None, None)
    return jax.shard_map(
        shards,
        mesh=mesh,
        in_specs=(data, data, data, data, P("uly", None), P("uly", None), P()),
        out_specs=(data, data, data),
        check_vma=False,
    )
```
